32 devices in a mesh: rx: 8 (over z, core), ry: 4 (over y, x).
Axes of the slice: x: 2, y: 2, z: 4, core: 2. Of those that a mesh axis runs over, the one named last changes fastest.
Arguments:
- record: bfloat16 [256, 256, 2048], P('rx', 'ry'), may hold values from -6 to 6
- sampled: int32 [256, 256], P('rx', 'ry'), may hold values 0 or 1
- levels: int32 [2], replicated, may hold values from 40 to 160
Outputs:
- restored: bfloat16 [256, 256, 2048], P('rx', 'ry')
The draws below stay inside these ranges and needn't reach their ends.
All inputs are finite; a program needn't handle non-finite values. No bound on the sum of `sampled` on one device may be relied on, other than what follows from the above.
Results may differ from the reference program's by a relative error of at most 0.0027.
Values may be sent and summed in bfloat16 or wider, within the bound.
A program may use at most 128 MiB of HBM per device.

```python
import math
import jax
import jax.numpy as jnp
from jax import lax

CX = 32
CY = 64
H = 16
NT = 2048
NF = 128
FLO = 8
ITERS = 2
RX = 256
RY = 256
N_RX = 8


def set_ends(values, key, least, top_value):
    index_at = [jax.random.randint(jax.random.fold_in(key, axis), (), 0, length) for axis, length in enumerate(values.shape)]
    widest = values.shape.index(max(values.shape))
    next_to = index_at[:widest] + [(index_at[widest] + 1) % values.shape[widest]] + index_at[widest + 1:]
    return values.at[tuple(index_at)].set(least).at[tuple(next_to)].set(top_value)


def steps_of(key, shape, split, low, top_value):
    def one(axis_at, shards_of):
        steps = jax.random.uniform(jax.random.fold_in(jax.random.fold_in(key, 6), axis_at), (shards_of,), jnp.float32, low / len(split), top_value / len(split))
        return jnp.repeat(jnp.exp(steps), shape[axis_at] // shards_of).reshape((-1,) + (1,) * (len(shape) - axis_at - 1))

    gain = one(*split[0])
    for cut in split[1:]:
        gain = gain * one(*cut)
    return gain


def noise(stream_key, shape, width, bound, cuts=(), dtype=jnp.bfloat16):
    entries = width * jax.random.normal(stream_key, shape, jnp.float32)
    if cuts:
        entries = entries * steps_of(stream_key, shape, cuts, -0.22, 0.18)
    return jnp.clip(entries, -bound, bound).astype(dtype)


def setup_inputs(seed: int = 0) -> dict:
    arg_keys = jax.random.split(jax.random.key(seed), 4)
    return {
        "record": noise(arg_keys[0], (RX, RY, NT), 1.0, 6.0, ((0, 8), (1, 4))),
        "sampled": set_ends((jax.random.randint(arg_keys[1], (RX, RY), 0, 2) < 1).astype(jnp.int32), jax.random.fold_in(arg_keys[1], 1), 0, 1),
        "levels": jax.random.randint(arg_keys[2], (ITERS,), 40, 161).astype(jnp.int32),
    }


def angles(row_ids, column_ids, period):
    products = row_ids[:, None] * column_ids[None, :] % period
    return products.astype(jnp.float32) * (2.0 * math.pi / period)

def taper(interior, margin):
    offsets = jnp.arange(interior + 2 * margin).astype(jnp.float32)
    rising = jnp.sin(0.5 * math.pi * (offsets + 0.5) / (2 * margin))
    falling = jnp.cos(0.5 * math.pi * (offsets - interior + 0.5) / (2 * margin))
    return jnp.where(offsets < 2 * margin, rising, jnp.where(offsets >= interior, falling, jnp.ones_like(offsets)))

def time_forward(samples, bin_ids):
    phases = angles(jnp.arange(samples), bin_ids, samples)
    return jnp.stack([jnp.cos(phases), -jnp.sin(phases)], axis=1).astype(jnp.bfloat16)

def time_inverse(samples, bin_ids):
    phases = angles(bin_ids, jnp.arange(samples), samples)
    factor = 2.0 / samples
    return jnp.stack([jnp.cos(phases) * factor, -jnp.sin(phases) * factor], axis=1).astype(jnp.bfloat16)

def tile_forward(interior, margin):
    length = interior + 2 * margin
    offsets = jnp.arange(length)
    phases = angles(offsets, offsets, length)
    weights = taper(interior, margin)[None, :]
    cosine = (weights * jnp.cos(phases)).astype(jnp.bfloat16)
    sine_table = (weights * jnp.sin(phases)).astype(jnp.bfloat16)
    real_rows = jnp.stack([cosine, sine_table], axis=1)
    imag_rows = jnp.stack([-sine_table, cosine], axis=1)
    return jnp.stack([real_rows, imag_rows], axis=0)

def tile_inverse(interior, margin):
    length = interior + 2 * margin
    offsets = jnp.arange(length)
    phases = angles(offsets, offsets, length)
    weights = (taper(interior, margin) * (1.0 / length))[:, None]
    cosine = (weights * jnp.cos(phases)).astype(jnp.bfloat16)
    sine_table = (weights * jnp.sin(phases)).astype(jnp.bfloat16)
    real_rows = jnp.stack([cosine, -sine_table], axis=1)
    imag_rows = jnp.stack([sine_table, cosine], axis=1)
    return jnp.stack([real_rows, imag_rows], axis=0)

def plane_forward(positions, halves, length):
    columns = jnp.arange(2 * length)
    phases = angles(positions, columns % length, length)
    matched = halves[:, None] == (columns // length)[None, :]
    signed = jnp.where(halves[:, None] == 0, -1.0, 1.0) * jnp.sin(phases)
    return jnp.where(matched, jnp.cos(phases), signed).astype(jnp.bfloat16)

def plane_inverse(positions, halves, length):
    rows_all = jnp.arange(2 * length)
    phases = angles(rows_all % length, positions, length)
    factor = 1.0 / length
    matched = (rows_all // length)[:, None] == halves[None, :]
    signed = jnp.where((rows_all // length)[:, None] == 0, 1.0, -1.0) * (jnp.sin(phases) * factor)
    return jnp.where(matched, jnp.cos(phases) * factor, signed).astype(jnp.bfloat16)

def intersection_add(pieces, interior, margin):
    middle = pieces[:, :, margin:margin + interior].astype(jnp.float32)
    from_left = jnp.roll(pieces[:, :, interior + margin:], 1, axis=1).astype(jnp.float32)
    from_right = jnp.roll(pieces[:, :, :margin], -1, axis=1).astype(jnp.float32)
    filler = jnp.zeros(middle.shape[:2] + (interior - 2 * margin,) + middle.shape[3:], jnp.float32)
    extra = jnp.concatenate([from_left, filler, from_right], axis=2)
    return (middle + extra).astype(jnp.bfloat16)

def reference(record, sampled, levels):
    bin_ids = FLO + jnp.arange(NF)
    forward_time = time_forward(NT, bin_ids).astype(jnp.float32)
    inverse_time = time_inverse(NT, bin_ids).astype(jnp.float32)
    forward_tile = tile_forward(CY, H).astype(jnp.float32)
    inverse_tile = tile_inverse(CY, H).astype(jnp.float32)
    positions = jnp.concatenate([jnp.arange(RX), jnp.arange(RX)])
    halves = jnp.concatenate([jnp.zeros(RX, jnp.int32), jnp.ones(RX, jnp.int32)])
    forward_plane = plane_forward(positions, halves, RX).astype(jnp.float32)
    inverse_plane = plane_inverse(positions, halves, RX).astype(jnp.float32)
    tiles_count = RY // CY
    length = CY + 2 * H
    current = jnp.where(sampled[:, :, None] > 0, record, jnp.zeros((), jnp.bfloat16))
    record_blocks = record.reshape(N_RX, CX, RY, NT)
    kept_blocks = sampled.astype(jnp.float32).reshape(N_RX, CX, RY, 1)

    def spectrum(row_block):
        return jnp.einsum('xyt,tpf->fypx', row_block.astype(jnp.float32), forward_time).astype(jnp.bfloat16)

    def rebuild(operands):
        column_piece, initial, kept = operands
        recon = jnp.einsum('fypx,fpt->xyt', column_piece.astype(jnp.float32), inverse_time)
        return (kept * initial.astype(jnp.float32) + (1.0 - kept) * recon).astype(jnp.bfloat16)
    for iteration in range(ITERS):
        spectra = lax.map(spectrum, current.reshape(N_RX, CX, RY, NT))
        spectra = jnp.transpose(spectra, (1, 2, 3, 0, 4)).reshape(NF, tiles_count, CY, 2, RX)
        leading = jnp.roll(spectra, 1, axis=1)[:, :, CY - H:]
        trailing = jnp.roll(spectra, -1, axis=1)[:, :, :H]
        windows = jnp.concatenate([leading, spectra, trailing], axis=2)
        turned = jnp.einsum('qkps,fjspx->fjkqx', forward_tile, windows.astype(jnp.float32)).astype(jnp.bfloat16)
        coeffs = jnp.dot(turned.reshape(-1, 2 * RX).astype(jnp.float32), forward_plane, preferred_element_type=jnp.float32)
        real_part = coeffs[:, :RX]
        imag_part = coeffs[:, RX:]
        magnitude = jnp.sqrt(real_part * real_part + imag_part * imag_part)
        largest = jnp.max(magnitude)
        cutoff = levels[iteration].astype(jnp.float32) * 0.001 * (largest + 1e-06)
        shrink = jnp.maximum(magnitude - cutoff, 0.0) / jnp.maximum(magnitude, cutoff)
        shrunk = (coeffs * jnp.concatenate([shrink, shrink], axis=1)).astype(jnp.bfloat16)
        planes = jnp.dot(shrunk.astype(jnp.float32), inverse_plane, preferred_element_type=jnp.float32)
        planes = planes.astype(jnp.bfloat16).reshape(NF, tiles_count, length, 2, RX)
        pieces = jnp.einsum('qspk,fjkpx->fjsqx', inverse_tile, planes.astype(jnp.float32)).astype(jnp.bfloat16)
        merged = intersection_add(pieces, CY, H).reshape(NF, RY, 2, N_RX, CX)
        column_pieces = jnp.moveaxis(merged, 3, 0)
        current = lax.map(rebuild, (column_pieces, record_blocks, kept_blocks)).reshape(RX, RY, NT)
    return current
```

```python
import functools
import math

import jax
import jax.numpy as jnp
import numpy as np
from jax import lax
from jax.experimental import pallas as pl
from jax.experimental.pallas import tpu as pltpu
from jax.sharding import PartitionSpec as P

H = 16
NF = 128
FLO = 8
ITERS = 2
LANES = 128
MISSING = float(2.0**100)
FOUND = float(2.0**90)
MESH = pl.DeviceIdType.MESH
VM = pl.BlockSpec(memory_space=pltpu.VMEM)
SM = pl.BlockSpec(memory_space=pltpu.SMEM)
ANY = pl.BlockSpec(memory_space=pl.ANY)


def rounded(table):
    return np.asarray(table, np.float32).astype(jnp.bfloat16)


def angles(rows, columns, period):
    return (rows[:, None] * columns[None, :] % period) * (2.0 * math.pi / period)


def time_table(samples, devices):
    share = NF // devices
    phases = angles(FLO + np.arange(NF), np.arange(samples), samples)
    both = np.stack([np.cos(phases), -np.sin(phases)]).reshape(2, devices, share, samples)
    return rounded(both.transpose(1, 0, 2, 3).reshape(2 * NF, samples))


def plane_tables(positions):
    length = positions.shape[0]
    phases = angles(np.arange(length), positions, length)
    c, s = np.cos(phases), np.sin(phases)
    forward = np.block([[c, s], [-s, c]])
    c, s = c.T / length, s.T / length
    inverse = np.block([[c, -s], [s, c]])
    return rounded(forward), rounded(inverse)


def tile_tables(interior, extent):
    length = interior + 2 * H
    tiles = extent // interior
    offsets = np.arange(length)
    taper = np.where(
        offsets < 2 * H,
        np.sin(0.5 * math.pi * (offsets + 0.5) / (2 * H)),
        np.where(offsets >= interior, np.cos(0.5 * math.pi * (offsets - interior + 0.5) / (2 * H)), 1.0),
    )
    phases = angles(offsets, offsets, length)
    c, s = np.cos(phases), np.sin(phases)
    forward = np.zeros((2, extent, 2, tiles, length))
    inverse = np.zeros((2, tiles, length, 2, extent))
    ya, yb = taper[:, None] * c, taper[:, None] * s
    yc, yd = c * (taper / length)[None, :], s * (taper / length)[None, :]
    for j in range(tiles):
        at = (j * interior - H + offsets) % extent
        for o in range(length):
            forward[0, at[o], 0, j] += ya[o]
            forward[1, at[o], 0, j] += yb[o]
            forward[0, at[o], 1, j] -= yb[o]
            forward[1, at[o], 1, j] += ya[o]
            inverse[0, j, :, 0, at[o]] += yc[:, o]
            inverse[1, j, :, 0, at[o]] -= yd[:, o]
            inverse[0, j, :, 1, at[o]] += yd[:, o]
            inverse[1, j, :, 1, at[o]] += yc[:, o]
    wide = 2 * tiles * length
    return rounded(forward.reshape(2 * extent, wide)), rounded(inverse.reshape(wide, 2 * extent))


def meet_all(across, down):
    devices = across * down
    me = lax.axis_index("rx") * down + lax.axis_index("ry")
    barrier = pltpu.get_barrier_semaphore()

    def greet(k, carry):
        peer = lax.rem(me + k, devices)
        pl.semaphore_signal(
            barrier, inc=1, device_id=(peer // down, lax.rem(peer, down)), device_id_type=MESH
        )
        return carry

    lax.fori_loop(1, devices, greet, 0)
    pl.semaphore_wait(barrier, devices - 1)
    return me


def exchange_kernel(across, down, per_peer, src, dst, send_sem, recv_sem, own_sem):
    devices = across * down
    me = meet_all(across, down)

    def outgoing(k):
        peer = lax.rem(me + k, devices)
        return pltpu.make_async_remote_copy(
            src_ref=src.at[peer] if per_peer else src,
            dst_ref=dst.at[me],
            send_sem=send_sem.at[peer],
            recv_sem=recv_sem.at[me],
            device_id=(peer // down, lax.rem(peer, down)),
            device_id_type=MESH,
        )

    def incoming(k):
        peer = lax.rem(me + k, devices)
        return pltpu.make_async_remote_copy(
            src_ref=src.at[peer] if per_peer else src,
            dst_ref=dst.at[peer],
            send_sem=send_sem.at[peer],
            recv_sem=recv_sem.at[peer],
            device_id=(peer // down, lax.rem(peer, down)),
            device_id_type=MESH,
        )

    def start(k, carry):
        outgoing(k).start()
        return carry

    def finish(k, carry):
        incoming(k).wait()
        return carry

    own = pltpu.make_async_copy(src.at[me] if per_peer else src, dst.at[me], own_sem)
    own.start()
    lax.fori_loop(1, devices, start, 0)
    own.wait()
    lax.fori_loop(1, devices, finish, 0)


def exchange(across, down, blocks, collective_id):
    devices = across * down
    return pl.pallas_call(
        functools.partial(exchange_kernel, across, down, True),
        out_shape=jax.ShapeDtypeStruct(blocks.shape, blocks.dtype),
        in_specs=[VM],
        out_specs=VM,
        scratch_shapes=[
            pltpu.SemaphoreType.DMA((devices,)),
            pltpu.SemaphoreType.DMA((devices,)),
            pltpu.SemaphoreType.DMA,
        ],
        compiler_params=pltpu.CompilerParams(collective_id=collective_id, has_side_effects=True),
    )(blocks)


def share_max(across, down, peaks):
    devices = across * down
    return pl.pallas_call(
        functools.partial(exchange_kernel, across, down, False),
        out_shape=jax.ShapeDtypeStruct((devices,) + peaks.shape, peaks.dtype),
        in_specs=[VM],
        out_specs=VM,
        scratch_shapes=[
            pltpu.SemaphoreType.DMA((devices,)),
            pltpu.SemaphoreType.DMA((devices,)),
            pltpu.SemaphoreType.DMA,
        ],
        compiler_params=pltpu.CompilerParams(collective_id=2, has_side_effects=True),
    )(peaks)


def dot(a, b):
    return jnp.dot(a, b, preferred_element_type=jnp.float32)


def analyse(sizes, grid, plane, tile, coeffs, peaks):
    nx, ny, share, half = sizes
    best = jnp.zeros((8, LANES), jnp.float32)
    for f in range(share):
        turned = dot(plane[...], grid[:, f * ny : (f + 1) * ny]).astype(jnp.bfloat16)
        c = dot(jnp.concatenate([turned[:nx], turned[nx:]], axis=1), tile[...])
        coeffs[f] = c
        re, im = c[:, :half], c[:, half:]
        power = re * re + im * im
        best = jnp.maximum(best, jnp.max(power.reshape(-1, 8, half), axis=0)[:, :LANES])
        for part in range(1, half // LANES):
            best = jnp.maximum(
                best,
                jnp.max(power[:, part * LANES : (part + 1) * LANES].reshape(-1, 8, LANES), axis=0),
            )
    peaks[...] = best


def synthesise(sizes, level, tops, coeffs, plane, tile):
    nx, ny, share, half = sizes
    largest = jnp.sqrt(jnp.max(jnp.max(tops[...], axis=0), keepdims=True))
    cutoff = level.astype(jnp.float32) * 0.001 * (largest + 1e-06)
    for f in range(share):
        re, im = coeffs[f, :, :half], coeffs[f, :, half:]
        magnitude = jnp.sqrt(re * re + im * im)
        shrink = jnp.maximum(magnitude - cutoff, 0.0) / jnp.maximum(magnitude, cutoff)
        shrunk = jnp.concatenate(
            [(re * shrink).astype(jnp.bfloat16), (im * shrink).astype(jnp.bfloat16)], axis=1
        )
        lines = dot(shrunk, tile[...]).astype(jnp.bfloat16)
        yield f, dot(plane[...], jnp.concatenate([lines[:, :ny], lines[:, ny:]], axis=0))


def first_kernel(sizes, shape, received, plane, tile, marked, coeffs, peaks, grid, left, right):
    across, down, interior, groups = shape
    nx, ny, share, half = sizes
    rows = 2 * share
    lower = lax.broadcasted_iota(jnp.int32, (groups, LANES), 1) < interior

    def gather(rx, carry):
        for pair in range(down // 2):
            for at, ref in ((0, left), (1, right)):
                block = received[rx * down + 2 * pair + at].astype(jnp.float32)
                for g in range(groups):
                    ref[g * rows : (g + 1) * rows] = block[:, g * LANES : (g + 1) * LANES]
            for r in range(rows):
                p, f = r // share, r % share
                a = left[pl.ds(r, groups, stride=rows)]
                b = right[pl.ds(r, groups, stride=rows)]
                first = jnp.where(lower, a, pltpu.roll(b, interior, 1)).astype(jnp.bfloat16)
                second = jnp.where(lower, pltpu.roll(a, interior, 1), b).astype(jnp.bfloat16)
                lanes = slice(f * ny + pair * LANES, f * ny + (pair + 1) * LANES)
                for xa, value in ((0, first), (1, second)):
                    row = pl.multiple_of(p * nx + (xa * across + rx) * groups, groups)
                    marked[pl.ds(row, groups), lanes] = value
        return carry

    lax.fori_loop(0, across, gather, 0)
    seen = marked[...].astype(jnp.float32)
    grid[...] = jnp.where(seen > FOUND, 0.0, seen).astype(jnp.bfloat16)
    analyse(sizes, grid, plane, tile, coeffs, peaks)


def again_kernel(
    sizes, iteration, levels, tops, old, marked, inv_tile, inv_plane, plane, tile, coeffs, peaks, grid
):
    nx, ny, share, half = sizes
    for f, back in synthesise(sizes, levels[iteration], tops, old, inv_plane, inv_tile):
        lanes = slice(f * ny, (f + 1) * ny)
        seen = marked[:, lanes].astype(jnp.float32)
        grid[:, lanes] = jnp.where(seen > FOUND, back, seen).astype(jnp.bfloat16)
    analyse(sizes, grid, plane, tile, coeffs, peaks)


def last_kernel(
    sizes, shape, iteration, levels, tops, old, inv_tile, inv_plane, sent, grid, left, right
):
    across, down, interior, groups = shape
    nx, ny, share, half = sizes
    rows = 2 * share
    for f, back in synthesise(sizes, levels[iteration], tops, old, inv_plane, inv_tile):
        grid[:, f * ny : (f + 1) * ny] = back
    lower = lax.broadcasted_iota(jnp.int32, (groups, LANES), 1) < interior

    def spread(rx, carry):
        for pair in range(down // 2):
            for r in range(rows):
                p, f = r // share, r % share
                lanes = slice(f * ny + pair * LANES, f * ny + (pair + 1) * LANES)
                first, second = (
                    grid[pl.ds(pl.multiple_of(p * nx + (xa * across + rx) * groups, groups), groups), lanes]
                    for xa in range(2)
                )
                left[pl.ds(r, groups, stride=rows)] = jnp.where(lower, first, pltpu.roll(second, interior, 1))
                right[pl.ds(r, groups, stride=rows)] = jnp.where(lower, pltpu.roll(first, interior, 1), second)
            for at, ref in ((0, left), (1, right)):
                for g in range(groups):
                    sent[rx * down + 2 * pair + at, :, g * LANES : (g + 1) * LANES] = ref[
                        g * rows : (g + 1) * rows
                    ].astype(jnp.bfloat16)
        return carry

    lax.fori_loop(0, across, spread, 0)


def body(across, down, record, sampled, levels):
    rows_x, rows_y, samples = record.shape
    devices = across * down
    share = NF // devices
    rows = 2 * share
    nx, ny = rows_x * across, rows_y * down
    traces = rows_x * rows_y
    pack = LANES // rows_y
    groups = traces // LANES
    assert pack == 2 and down % 2 == 0
    half = ny // rows_y * (rows_y + 2 * H)
    sizes = (nx, ny, share, half)
    shape = (across, down, rows_y, groups)
    times = jnp.asarray(time_table(samples, devices))
    ids = np.arange(nx)
    xa, rx, g = ids // (across * groups), ids // groups % across, ids % groups
    plane, inv_plane = map(jnp.asarray, plane_tables(rx * rows_x + g * pack + xa))
    tile, inv_tile = map(jnp.asarray, tile_tables(rows_y, ny))
    flat = record.reshape(traces, samples)
    spectra = lax.dot_general(
        times, flat, (((1,), (1,)), ((), ())), preferred_element_type=jnp.float32
    )
    spectra = jnp.where(sampled.reshape(1, traces) > 0, spectra, MISSING).astype(jnp.bfloat16)
    received = exchange(across, down, spectra.reshape(devices, rows, traces), 0)
    coeffs_type = jax.ShapeDtypeStruct((share, nx, 2 * half), jnp.float32)
    peaks_type = jax.ShapeDtypeStruct((8, LANES), jnp.float32)
    grid_shape = (2 * nx, share * ny)
    folded = [pltpu.VMEM((groups * rows, LANES), jnp.float32)] * 2
    params = pltpu.CompilerParams(vmem_limit_bytes=48 * 1024 * 1024)
    marked, coeffs, peaks = pl.pallas_call(
        functools.partial(first_kernel, sizes, shape),
        out_shape=(jax.ShapeDtypeStruct(grid_shape, jnp.bfloat16), coeffs_type, peaks_type),
        in_specs=[VM] * 3,
        out_specs=(VM,) * 3,
        scratch_shapes=[pltpu.VMEM(grid_shape, jnp.bfloat16)] + folded,
        compiler_params=params,
    )(received, plane, tile)
    for iteration in range(ITERS - 1):
        tops = share_max(across, down, peaks)
        coeffs, peaks = pl.pallas_call(
            functools.partial(again_kernel, sizes, iteration),
            out_shape=(coeffs_type, peaks_type),
            in_specs=[SM] + [VM] * 7,
            out_specs=(VM,) * 2,
            scratch_shapes=[pltpu.VMEM(grid_shape, jnp.bfloat16)],
            compiler_params=params,
        )(levels, tops, coeffs, marked, inv_tile, inv_plane, plane, tile)
    tops = share_max(across, down, peaks)
    sent = pl.pallas_call(
        functools.partial(last_kernel, sizes, shape, ITERS - 1),
        out_shape=jax.ShapeDtypeStruct((devices, rows, traces), jnp.bfloat16),
        in_specs=[SM] + [VM] * 4,
        out_specs=VM,
        scratch_shapes=[pltpu.VMEM(grid_shape, jnp.float32)] + folded,
        compiler_params=params,
    )(levels, tops, coeffs, inv_tile, inv_plane)
    returned = exchange(across, down, sent, 1)
    recon = lax.dot_general(
        returned.reshape(2 * NF, traces), times, (((0,), (0,)), ((), ())),
        preferred_element_type=jnp.float32,
    ).reshape(rows_x, rows_y, samples) * (2.0 / samples)
    return jnp.where(sampled[:, :, None] > 0, record.astype(jnp.float32), recon).astype(jnp.bfloat16)


def solution(mesh):
    return jax.shard_map(
        functools.partial(body, mesh.shape["rx"], mesh.shape["ry"]),
        mesh=mesh,
        in_specs=(P("rx", "ry", None), P("rx", "ry"), P()),
        out_specs=P("rx", "ry", None),
        check_vma=False,
    )
```

```python
import functools
import math

import jax
import jax.numpy as jnp
import numpy as np
from jax import lax
from jax.experimental import pallas as pl
from jax.experimental.pallas import tpu as pltpu
from jax.sharding import PartitionSpec as P

H = 16
NF = 128
FLO = 8
ITERS = 2
LANES = 128
MISSING = float(2.0**100)
FOUND = float(2.0**90)
MESH = pl.DeviceIdType.MESH
VM = pl.BlockSpec(memory_space=pltpu.VMEM)
SM = pl.BlockSpec(memory_space=pltpu.SMEM)
ANY = pl.BlockSpec(memory_space=pl.ANY)


def rounded(table):
    return np.asarray(table, np.float32).astype(jnp.bfloat16)


def angles(rows, columns, period):
    return (rows[:, None] * columns[None, :] % period) * (2.0 * math.pi / period)


def time_table(samples, devices):
    share = NF // devices
    phases = angles(FLO + np.arange(NF), np.arange(samples), samples)
    both = np.stack([np.cos(phases), -np.sin(phases)]).reshape(2, devices, share, samples)
    return rounded(both.transpose(1, 0, 2, 3).reshape(2 * NF, samples))


def plane_tables(positions):
    length = positions.shape[0]
    phases = angles(np.arange(length), positions, length)
    c, s = np.cos(phases), np.sin(phases)
    forward = np.block([[c, s], [-s, c]])
    c, s = c.T / length, s.T / length
    inverse = np.block([[c, -s], [s, c]])
    return rounded(forward), rounded(inverse)


def tile_tables(interior, extent):
    length = interior + 2 * H
    tiles = extent // interior
    offsets = np.arange(length)
    taper = np.where(
        offsets < 2 * H,
        np.sin(0.5 * math.pi * (offsets + 0.5) / (2 * H)),
        np.where(offsets >= interior, np.cos(0.5 * math.pi * (offsets - interior + 0.5) / (2 * H)), 1.0),
    )
    phases = angles(offsets, offsets, length)
    c, s = np.cos(phases), np.sin(phases)
    forward = np.zeros((2, extent, 2, tiles, length))
    inverse = np.zeros((2, tiles, length, 2, extent))
    ya, yb = taper[:, None] * c, taper[:, None] * s
    yc, yd = c * (taper / length)[None, :], s * (taper / length)[None, :]
    for j in range(tiles):
        at = (j * interior - H + offsets) % extent
        for o in range(length):
            forward[0, at[o], 0, j] += ya[o]
            forward[1, at[o], 0, j] += yb[o]
            forward[0, at[o], 1, j] -= yb[o]
            forward[1, at[o], 1, j] += ya[o]
            inverse[0, j, :, 0, at[o]] += yc[:, o]
            inverse[1, j, :, 0, at[o]] -= yd[:, o]
            inverse[0, j, :, 1, at[o]] += yd[:, o]
            inverse[1, j, :, 1, at[o]] += yc[:, o]
    wide = 2 * tiles * length
    return rounded(forward.reshape(2 * extent, wide)), rounded(inverse.reshape(wide, 2 * extent))


def greet_all(across, down, me):
    devices = across * down

    def greet(k, carry):
        peer = lax.rem(me + k, devices)
        pl.semaphore_signal(
            pltpu.get_barrier_semaphore(),
            inc=1,
            device_id=(peer // down, lax.rem(peer, down)),
            device_id_type=MESH,
        )
        return carry

    lax.fori_loop(1, devices, greet, 0)


def remote(down, peer, src, dst, send_sem, recv_sem):
    return pltpu.make_async_remote_copy(
        src_ref=src,
        dst_ref=dst,
        send_sem=send_sem,
        recv_sem=recv_sem,
        device_id=(peer // down, lax.rem(peer, down)),
        device_id_type=MESH,
    )


def dot(a, b):
    return jnp.dot(a, b, preferred_element_type=jnp.float32)


def analyse(sizes, grid, plane, tile, coeffs, peak):
    nx, ny, share, half = sizes
    best = jnp.zeros((8, LANES), jnp.float32)
    for f in range(share):
        turned = dot(plane[...], grid[:, f * ny : (f + 1) * ny]).astype(jnp.bfloat16)
        c = dot(jnp.concatenate([turned[:nx], turned[nx:]], axis=1), tile[...])
        coeffs[f] = c
        re, im = c[:, :half], c[:, half:]
        power = re * re + im * im
        best = jnp.maximum(best, jnp.max(power.reshape(-1, 8, half), axis=0)[:, :LANES])
        for part in range(1, half // LANES):
            best = jnp.maximum(
                best,
                jnp.max(power[:, part * LANES : (part + 1) * LANES].reshape(-1, 8, LANES), axis=0),
            )
    peak[...] = jnp.max(best, axis=0, keepdims=True)


def synthesise(sizes, level, tops, coeffs, plane, tile):
    nx, ny, share, half = sizes
    largest = jnp.sqrt(jnp.max(jnp.max(tops[...], axis=0), keepdims=True))
    cutoff = level.astype(jnp.float32) * 0.001 * (largest + 1e-06)
    for f in range(share):
        re, im = coeffs[f, :, :half], coeffs[f, :, half:]
        magnitude = jnp.sqrt(re * re + im * im)
        shrink = jnp.maximum(magnitude - cutoff, 0.0) / jnp.maximum(magnitude, cutoff)
        shrunk = jnp.concatenate(
            [(re * shrink).astype(jnp.bfloat16), (im * shrink).astype(jnp.bfloat16)], axis=1
        )
        lines = dot(shrunk, tile[...]).astype(jnp.bfloat16)
        yield f, dot(plane[...], jnp.concatenate([lines[:, :ny], lines[:, ny:]], axis=0))


def whole_kernel(
    sizes, shape, levels, spectra, plane, tile, inv_plane, inv_tile, returned,
    received, marked, grid, rebuilt, coeffs, peaks, tops, sent, left, right,
    out_send, out_recv, top_send, top_recv, back_send, back_recv, own_sem,
):
    across, down, interior, groups = shape
    nx, ny, share, half = sizes
    rows = 2 * share
    devices = across * down
    my_x, my_y = lax.axis_index("rx"), lax.axis_index("ry")
    me = my_x * down + my_y
    lower = lax.broadcasted_iota(jnp.int32, (groups, LANES), 1) < interior
    greet_all(across, down, me)
    pl.semaphore_wait(pltpu.get_barrier_semaphore(), devices - 1)

    def out_copy(peer, slot):
        return remote(down, peer, spectra.at[peer], received.at[slot], out_send.at[peer], out_recv.at[slot])

    def back_copy(peer, slot):
        return remote(down, peer, sent.at[peer], returned.at[slot], back_send.at[peer], back_recv.at[slot])

    def top_copy(iteration, peer, slot):
        return remote(
            down, peer, peaks.at[iteration], tops.at[iteration, slot],
            top_send.at[iteration, peer], top_recv.at[iteration, slot],
        )

    def send_out(k, carry):
        peer = lax.rem(my_x + k // down, across) * down + lax.rem(my_y + k % down, down)

        @pl.when(peer != me)
        def _():
            out_copy(peer, me).start()

        return carry

    lax.fori_loop(0, devices, send_out, 0)
    received[me] = spectra[me]

    def gather(k, carry):
        rx = lax.rem(my_x + across - k, across)
        for ry in range(down):
            peer = rx * down + ry

            @pl.when(peer != me)
            def _():
                out_copy(peer, peer).wait_recv()

        for pair in range(down // 2):
            for at, ref in ((0, left), (1, right)):
                block = received[rx * down + 2 * pair + at].astype(jnp.float32)
                for g in range(groups):
                    ref[g * rows : (g + 1) * rows] = block[:, g * LANES : (g + 1) * LANES]
            for r in range(rows):
                p, f = r // share, r % share
                a = left[pl.ds(r, groups, stride=rows)]
                b = right[pl.ds(r, groups, stride=rows)]
                first = jnp.where(lower, a, pltpu.roll(b, interior, 1)).astype(jnp.bfloat16)
                second = jnp.where(lower, pltpu.roll(a, interior, 1), b).astype(jnp.bfloat16)
                lanes = slice(f * ny + pair * LANES, f * ny + (pair + 1) * LANES)
                for xa, value in ((0, first), (1, second)):
                    row = pl.multiple_of(p * nx + (xa * across + rx) * groups, groups)
                    marked[pl.ds(row, groups), lanes] = value
        return carry

    lax.fori_loop(0, across, gather, 0)
    for iteration in range(ITERS):
        for f in range(share):
            lanes = slice(f * ny, (f + 1) * ny)
            seen = marked[:, lanes].astype(jnp.float32)
            other = rebuilt[:, lanes] if iteration else 0.0
            grid[:, lanes] = jnp.where(seen > FOUND, other, seen).astype(jnp.bfloat16)
        analyse(sizes, grid, plane, tile, coeffs, peaks.at[iteration])

        def send_top(k, carry):
            top_copy(iteration, lax.rem(me + k, devices), me).start()
            return carry

        def wait_top(k, carry):
            peer = lax.rem(me + k, devices)
            top_copy(iteration, peer, peer).wait()
            return carry

        lax.fori_loop(1, devices, send_top, 0)
        tops[iteration, me] = peaks[iteration]
        lax.fori_loop(1, devices, wait_top, 0)
        for f, back in synthesise(sizes, levels[iteration], tops.at[iteration], coeffs, inv_plane, inv_tile):
            rebuilt[:, f * ny : (f + 1) * ny] = back

    def spread(k, carry):
        rx = lax.rem(my_x + k, across)
        for pair in range(down // 2):
            for r in range(rows):
                p, f = r // share, r % share
                lanes = slice(f * ny + pair * LANES, f * ny + (pair + 1) * LANES)
                first, second = (
                    rebuilt[pl.ds(pl.multiple_of(p * nx + (xa * across + rx) * groups, groups), groups), lanes]
                    for xa in range(2)
                )
                left[pl.ds(r, groups, stride=rows)] = jnp.where(lower, first, pltpu.roll(second, interior, 1))
                right[pl.ds(r, groups, stride=rows)] = jnp.where(lower, pltpu.roll(first, interior, 1), second)
            for at, ref in ((0, left), (1, right)):
                for g in range(groups):
                    sent[rx * down + 2 * pair + at, :, g * LANES : (g + 1) * LANES] = ref[
                        g * rows : (g + 1) * rows
                    ].astype(jnp.bfloat16)
        for ry in range(down):
            peer = rx * down + ry

            @pl.when(peer != me)
            def _():
                back_copy(peer, me).start()

        return carry

    lax.fori_loop(0, across, spread, 0)
    own = pltpu.make_async_copy(sent.at[me], returned.at[me], own_sem)
    own.start()
    own.wait()

    def finish(k, carry):
        peer = lax.rem(me + k, devices)
        out_copy(peer, peer).wait_send()
        back_copy(peer, peer).wait()
        return carry

    lax.fori_loop(1, devices, finish, 0)


def body(across, down, record, sampled, levels):
    rows_x, rows_y, samples = record.shape
    devices = across * down
    share = NF // devices
    rows = 2 * share
    nx, ny = rows_x * across, rows_y * down
    traces = rows_x * rows_y
    pack = LANES // rows_y
    groups = traces // LANES
    assert pack == 2 and down % 2 == 0
    half = ny // rows_y * (rows_y + 2 * H)
    sizes = (nx, ny, share, half)
    shape = (across, down, rows_y, groups)
    times = jnp.asarray(time_table(samples, devices))
    ids = np.arange(nx)
    xa, rx, g = ids // (across * groups), ids // groups % across, ids % groups
    plane, inv_plane = map(jnp.asarray, plane_tables(rx * rows_x + g * pack + xa))
    tile, inv_tile = map(jnp.asarray, tile_tables(rows_y, ny))
    flat = record.reshape(traces, samples)
    spectra = lax.dot_general(
        times, flat, (((1,), (1,)), ((), ())), preferred_element_type=jnp.float32
    )
    spectra = jnp.where(sampled.reshape(1, traces) > 0, spectra, MISSING).astype(jnp.bfloat16)
    block_shape = (devices, rows, traces)
    grid_shape = (2 * nx, share * ny)
    sem = pltpu.SemaphoreType.DMA
    returned = pl.pallas_call(
        functools.partial(whole_kernel, sizes, shape),
        out_shape=jax.ShapeDtypeStruct(block_shape, jnp.bfloat16),
        in_specs=[SM] + [VM] * 5,
        out_specs=VM,
        scratch_shapes=[
            pltpu.VMEM(block_shape, jnp.bfloat16),
            pltpu.VMEM(grid_shape, jnp.bfloat16),
            pltpu.VMEM(grid_shape, jnp.bfloat16),
            pltpu.VMEM(grid_shape, jnp.float32),
            pltpu.VMEM((share, nx, 2 * half), jnp.float32),
            pltpu.VMEM((ITERS, 1, LANES), jnp.float32),
            pltpu.VMEM((ITERS, devices, 1, LANES), jnp.float32),
            pltpu.VMEM(block_shape, jnp.bfloat16),
            pltpu.VMEM((groups * rows, LANES), jnp.float32),
            pltpu.VMEM((groups * rows, LANES), jnp.float32),
            sem((devices,)),
            sem((devices,)),
            sem((ITERS, devices)),
            sem((ITERS, devices)),
            sem((devices,)),
            sem((devices,)),
            sem,
        ],
        compiler_params=pltpu.CompilerParams(
            collective_id=0, has_side_effects=True, vmem_limit_bytes=48 * 1024 * 1024
        ),
    )(levels, spectra.reshape(block_shape), plane, tile, inv_plane, inv_tile)
    recon = lax.dot_general(
        returned.reshape(2 * NF, traces), times, (((0,), (0,)), ((), ())),
        preferred_element_type=jnp.float32,
    ).reshape(rows_x, rows_y, samples) * (2.0 / samples)
    return jnp.where(sampled[:, :, None] > 0, record.astype(jnp.float32), recon).astype(jnp.bfloat16)


def solution(mesh):
    return jax.shard_map(
        functools.partial(body, mesh.shape["rx"], mesh.shape["ry"]),
        mesh=mesh,
        in_specs=(P("rx", "ry", None), P("rx", "ry"), P()),
        out_specs=P("rx", "ry", None),
        check_vma=False,
    )
```

```python
import functools
import math

import jax
import jax.numpy as jnp
import numpy as np
from jax import lax
from jax.experimental import pallas as pl
from jax.experimental.pallas import tpu as pltpu
from jax.sharding import PartitionSpec as P

H = 16
NF = 128
FLO = 8
ITERS = 2
LANES = 128
LOADS = 4
SENDS = 2
MISSING = float(2.0**100)
FOUND = float(2.0**90)
MESH = pl.DeviceIdType.MESH
VM = pl.BlockSpec(memory_space=pltpu.VMEM)
SM = pl.BlockSpec(memory_space=pltpu.SMEM)
ANY = pl.BlockSpec(memory_space=pl.ANY)


def rounded(table):
    return np.asarray(table, np.float32).astype(jnp.bfloat16)


def angles(rows, columns, period):
    return (rows[:, None] * columns[None, :] % period) * (2.0 * math.pi / period)


def time_table(samples, devices):
    share = NF // devices
    phases = angles(FLO + np.arange(NF), np.arange(samples), samples)
    both = np.stack([np.cos(phases), -np.sin(phases)]).reshape(2, devices, share, samples)
    return rounded(both.transpose(1, 0, 2, 3).reshape(2 * NF, samples))


def plane_tables(positions):
    length = positions.shape[0]
    phases = angles(np.arange(length), positions, length)
    c, s = np.cos(phases), np.sin(phases)
    forward = np.block([[c, s], [-s, c]])
    c, s = c.T / length, s.T / length
    inverse = np.block([[c, -s], [s, c]])
    return rounded(forward), rounded(inverse)


def tile_tables(interior, extent):
    length = interior + 2 * H
    tiles = extent // interior
    offsets = np.arange(length)
    taper = np.where(
        offsets < 2 * H,
        np.sin(0.5 * math.pi * (offsets + 0.5) / (2 * H)),
        np.where(offsets >= interior, np.cos(0.5 * math.pi * (offsets - interior + 0.5) / (2 * H)), 1.0),
    )
    phases = angles(offsets, offsets, length)
    c, s = np.cos(phases), np.sin(phases)
    forward = np.zeros((2, extent, 2, tiles, length))
    inverse = np.zeros((2, tiles, length, 2, extent))
    ya, yb = taper[:, None] * c, taper[:, None] * s
    yc, yd = c * (taper / length)[None, :], s * (taper / length)[None, :]
    for j in range(tiles):
        at = (j * interior - H + offsets) % extent
        for o in range(length):
            forward[0, at[o], 0, j] += ya[o]
            forward[1, at[o], 0, j] += yb[o]
            forward[0, at[o], 1, j] -= yb[o]
            forward[1, at[o], 1, j] += ya[o]
            inverse[0, j, :, 0, at[o]] += yc[:, o]
            inverse[1, j, :, 0, at[o]] -= yd[:, o]
            inverse[0, j, :, 1, at[o]] += yd[:, o]
            inverse[1, j, :, 1, at[o]] += yc[:, o]
    wide = 2 * tiles * length
    return rounded(forward.reshape(2 * extent, wide)), rounded(inverse.reshape(wide, 2 * extent))


def greet_all(across, down, me):
    devices = across * down

    def greet(k, carry):
        peer = lax.rem(me + k, devices)
        pl.semaphore_signal(
            pltpu.get_barrier_semaphore(),
            inc=1,
            device_id=(peer // down, lax.rem(peer, down)),
            device_id_type=MESH,
        )
        return carry

    lax.fori_loop(1, devices, greet, 0)


def remote(down, peer, src, dst, send_sem, recv_sem):
    return pltpu.make_async_remote_copy(
        src_ref=src,
        dst_ref=dst,
        send_sem=send_sem,
        recv_sem=recv_sem,
        device_id=(peer // down, lax.rem(peer, down)),
        device_id_type=MESH,
    )


def dot(a, b):
    return jnp.dot(a, b, preferred_element_type=jnp.float32)


def analyse(sizes, grid, plane, tile, coeffs, peak):
    nx, ny, share, half = sizes
    best = jnp.zeros((8, LANES), jnp.float32)
    for f in range(share):
        turned = dot(plane[...], grid[:, f * ny : (f + 1) * ny]).astype(jnp.bfloat16)
        c = dot(jnp.concatenate([turned[:nx], turned[nx:]], axis=1), tile[...])
        coeffs[f] = c
        re, im = c[:, :half], c[:, half:]
        power = re * re + im * im
        best = jnp.maximum(best, jnp.max(power.reshape(-1, 8, half), axis=0)[:, :LANES])
        for part in range(1, half // LANES):
            best = jnp.maximum(
                best,
                jnp.max(power[:, part * LANES : (part + 1) * LANES].reshape(-1, 8, LANES), axis=0),
            )
    peak[...] = jnp.max(best, axis=0, keepdims=True)


def synthesise(sizes, level, tops, coeffs, plane, tile):
    nx, ny, share, half = sizes
    largest = jnp.sqrt(jnp.max(jnp.max(tops[...], axis=0), keepdims=True))
    cutoff = level.astype(jnp.float32) * 0.001 * (largest + 1e-06)
    for f in range(share):
        re, im = coeffs[f, :, :half], coeffs[f, :, half:]
        magnitude = jnp.sqrt(re * re + im * im)
        shrink = jnp.maximum(magnitude - cutoff, 0.0) / jnp.maximum(magnitude, cutoff)
        shrunk = jnp.concatenate(
            [(re * shrink).astype(jnp.bfloat16), (im * shrink).astype(jnp.bfloat16)], axis=1
        )
        lines = dot(shrunk, tile[...]).astype(jnp.bfloat16)
        yield f, dot(plane[...], jnp.concatenate([lines[:, :ny], lines[:, ny:]], axis=0))


def whole_kernel(
    sizes, shape, levels, record, kept, times, plane, tile, inv_plane, inv_tile, returned,
    samples, spectra, received, marked, grid, rebuilt, coeffs, peaks, tops, sent, left, right,
    out_send, out_recv, top_send, top_recv, back_send, back_recv, own_sem, load_sem,
):
    across, down, interior, groups = shape
    nx, ny, share, half = sizes
    rows = 2 * share
    devices = across * down
    my_x, my_y = lax.axis_index("rx"), lax.axis_index("ry")
    me = my_x * down + my_y
    lower = lax.broadcasted_iota(jnp.int32, (groups, LANES), 1) < interior
    traces = groups * LANES
    loads, piece = samples.shape[:2]
    per_send = loads // SENDS
    part = traces // SENDS

    def load(c):
        return pltpu.make_async_copy(record.at[pl.ds(c * piece, piece)], samples.at[c], load_sem.at[c])

    for c in range(loads):
        load(c).start()
    greet_all(across, down, me)

    def out_copy(h, peer, slot):
        lanes = pl.ds(h * part, part)
        return remote(
            down, peer, spectra.at[peer, :, lanes], received.at[slot, :, lanes],
            out_send.at[h, peer], out_recv.at[h, slot],
        )

    def back_copy(peer, slot):
        return remote(down, peer, sent.at[peer], returned.at[slot], back_send.at[peer], back_recv.at[slot])

    def top_copy(iteration, peer, slot):
        return remote(
            down, peer, peaks.at[iteration], tops.at[iteration, slot],
            top_send.at[iteration, peer], top_recv.at[iteration, slot],
        )

    for h in range(SENDS):
        for c in range(h * per_send, (h + 1) * per_send):
            lanes = slice(c * piece, (c + 1) * piece)
            load(c).wait()
            lines = lax.dot_general(
                times[...], samples[c], (((1,), (1,)), ((), ())), preferred_element_type=jnp.float32
            )
            lines = jnp.where(kept[:, lanes] > 0, lines, MISSING)
            for d in range(devices):
                spectra[d, :, lanes] = lines[d * rows : (d + 1) * rows].astype(jnp.bfloat16)
        if h == 0:
            pl.semaphore_wait(pltpu.get_barrier_semaphore(), devices - 1)

        def send_out(k, carry):
            peer = lax.rem(my_x + k // down, across) * down + lax.rem(my_y + k % down, down)

            @pl.when(peer != me)
            def _():
                out_copy(h, peer, me).start()

            return carry

        lax.fori_loop(0, devices, send_out, 0)
    received[me] = spectra[me]

    def gather(k, carry):
        rx = lax.rem(my_x + across - k, across)
        for ry in range(down):
            peer = rx * down + ry

            @pl.when(peer != me)
            def _():
                for h in range(SENDS):
                    out_copy(h, peer, peer).wait_recv()

        for pair in range(down // 2):
            for at, ref in ((0, left), (1, right)):
                block = received[rx * down + 2 * pair + at].astype(jnp.float32)
                for g in range(groups):
                    ref[g * rows : (g + 1) * rows] = block[:, g * LANES : (g + 1) * LANES]
            for r in range(rows):
                p, f = r // share, r % share
                a = left[pl.ds(r, groups, stride=rows)]
                b = right[pl.ds(r, groups, stride=rows)]
                first = jnp.where(lower, a, pltpu.roll(b, interior, 1)).astype(jnp.bfloat16)
                second = jnp.where(lower, pltpu.roll(a, interior, 1), b).astype(jnp.bfloat16)
                lanes = slice(f * ny + pair * LANES, f * ny + (pair + 1) * LANES)
                for xa, value in ((0, first), (1, second)):
                    row = pl.multiple_of(p * nx + (xa * across + rx) * groups, groups)
                    marked[pl.ds(row, groups), lanes] = value
        return carry

    lax.fori_loop(0, across, gather, 0)
    for iteration in range(ITERS):
        for f in range(share):
            lanes = slice(f * ny, (f + 1) * ny)
            seen = marked[:, lanes].astype(jnp.float32)
            other = rebuilt[:, lanes] if iteration else 0.0
            grid[:, lanes] = jnp.where(seen > FOUND, other, seen).astype(jnp.bfloat16)
        analyse(sizes, grid, plane, tile, coeffs, peaks.at[iteration])

        def send_top(k, carry):
            top_copy(iteration, lax.rem(me + k, devices), me).start()
            return carry

        def wait_top(k, carry):
            peer = lax.rem(me + k, devices)
            top_copy(iteration, peer, peer).wait()
            return carry

        lax.fori_loop(1, devices, send_top, 0)
        tops[iteration, me] = peaks[iteration]
        lax.fori_loop(1, devices, wait_top, 0)
        for f, back in synthesise(sizes, levels[iteration], tops.at[iteration], coeffs, inv_plane, inv_tile):
            rebuilt[:, f * ny : (f + 1) * ny] = back

    def spread(k, carry):
        rx = lax.rem(my_x + k, across)
        for pair in range(down // 2):
            for r in range(rows):
                p, f = r // share, r % share
                lanes = slice(f * ny + pair * LANES, f * ny + (pair + 1) * LANES)
                first, second = (
                    rebuilt[pl.ds(pl.multiple_of(p * nx + (xa * across + rx) * groups, groups), groups), lanes]
                    for xa in range(2)
                )
                left[pl.ds(r, groups, stride=rows)] = jnp.where(lower, first, pltpu.roll(second, interior, 1))
                right[pl.ds(r, groups, stride=rows)] = jnp.where(lower, pltpu.roll(first, interior, 1), second)
            for at, ref in ((0, left), (1, right)):
                for g in range(groups):
                    sent[rx * down + 2 * pair + at, :, g * LANES : (g + 1) * LANES] = ref[
                        g * rows : (g + 1) * rows
                    ].astype(jnp.bfloat16)
        for ry in range(down):
            peer = rx * down + ry

            @pl.when(peer != me)
            def _():
                back_copy(peer, me).start()

        return carry

    lax.fori_loop(0, across, spread, 0)
    own = pltpu.make_async_copy(sent.at[me], returned.at[me], own_sem)
    own.start()
    own.wait()

    def finish(k, carry):
        peer = lax.rem(me + k, devices)
        for h in range(SENDS):
            out_copy(h, peer, peer).wait_send()
        back_copy(peer, peer).wait()
        return carry

    lax.fori_loop(1, devices, finish, 0)


def body(across, down, record, sampled, levels):
    rows_x, rows_y, samples = record.shape
    devices = across * down
    share = NF // devices
    rows = 2 * share
    nx, ny = rows_x * across, rows_y * down
    traces = rows_x * rows_y
    pack = LANES // rows_y
    groups = traces // LANES
    assert pack == 2 and down % 2 == 0
    half = ny // rows_y * (rows_y + 2 * H)
    sizes = (nx, ny, share, half)
    shape = (across, down, rows_y, groups)
    times = jnp.asarray(time_table(samples, devices))
    ids = np.arange(nx)
    xa, rx, g = ids // (across * groups), ids // groups % across, ids % groups
    plane, inv_plane = map(jnp.asarray, plane_tables(rx * rows_x + g * pack + xa))
    tile, inv_tile = map(jnp.asarray, tile_tables(rows_y, ny))
    flat = record.reshape(traces, samples)
    block_shape = (devices, rows, traces)
    grid_shape = (2 * nx, share * ny)
    sem = pltpu.SemaphoreType.DMA
    returned = pl.pallas_call(
        functools.partial(whole_kernel, sizes, shape),
        out_shape=jax.ShapeDtypeStruct(block_shape, jnp.bfloat16),
        in_specs=[SM, ANY] + [VM] * 6,
        out_specs=VM,
        scratch_shapes=[
            pltpu.VMEM((LOADS, traces // LOADS, samples), jnp.bfloat16),
            pltpu.VMEM(block_shape, jnp.bfloat16),
            pltpu.VMEM(block_shape, jnp.bfloat16),
            pltpu.VMEM(grid_shape, jnp.bfloat16),
            pltpu.VMEM(grid_shape, jnp.bfloat16),
            pltpu.VMEM(grid_shape, jnp.float32),
            pltpu.VMEM((share, nx, 2 * half), jnp.float32),
            pltpu.VMEM((ITERS, 1, LANES), jnp.float32),
            pltpu.VMEM((ITERS, devices, 1, LANES), jnp.float32),
            pltpu.VMEM(block_shape, jnp.bfloat16),
            pltpu.VMEM((groups * rows, LANES), jnp.float32),
            pltpu.VMEM((groups * rows, LANES), jnp.float32),
            sem((SENDS, devices)),
            sem((SENDS, devices)),
            sem((ITERS, devices)),
            sem((ITERS, devices)),
            sem((devices,)),
            sem((devices,)),
            sem,
            sem((LOADS,)),
        ],
        compiler_params=pltpu.CompilerParams(
            collective_id=0, has_side_effects=True, vmem_limit_bytes=48 * 1024 * 1024
        ),
    )(levels, flat, sampled.reshape(1, traces), times, plane, tile, inv_plane, inv_tile)
    recon = lax.dot_general(
        returned.reshape(2 * NF, traces), times, (((0,), (0,)), ((), ())),
        preferred_element_type=jnp.float32,
    ).reshape(rows_x, rows_y, samples) * (2.0 / samples)
    return jnp.where(sampled[:, :, None] > 0, record.astype(jnp.float32), recon).astype(jnp.bfloat16)


def solution(mesh):
    return jax.shard_map(
        functools.partial(body, mesh.shape["rx"], mesh.shape["ry"]),
        mesh=mesh,
        in_specs=(P("rx", "ry", None), P("rx", "ry"), P()),
        out_specs=P("rx", "ry", None),
        check_vma=False,
    )
```
